32 devices in a mesh: row: 8 (over z, y), col: 4 (over x, core).
Axes of the slice: x: 2, y: 2, z: 4, core: 2. Of those that a mesh axis runs over, the one named last changes fastest.
Arguments:
- start_block: float32 [64, 16, 128], P(('row', 'col')), may hold values from -6 to 6
- blocks: float32 [8, 4, 58, 128, 128], P('row', 'col'), as said below
- slot_row: int32 [8, 4, 58], P('row', 'col'), may hold values from 0 to 7, as said below
- slot_col: int32 [8, 4, 58], P('row', 'col'), may hold values from 0 to 15, as said below
- counts: int32 [8, 4], P('row', 'col'), may hold values from 34 to 58, as said below
Outputs:
- alphas: float32 [2, 16, 16], replicated
- betas: float32 [2, 16, 16], replicated
- next_block: float32 [64, 16, 128], P(('row', 'col'))
The draws below stay inside these ranges and needn't reach their ends.
Inputs may be any that keep to these rules, and one draw needn't show every extreme that they name: `blocks`: over all cells the live slots list each nonzero block of a symmetric matrix exactly once: block (J, I) is listed exactly when (I, J) is, holding its transpose. Slots at or past a cell's count hold finite values that are no part of H. `counts`: live slots of a cell come first; in every draw some cell has all 58 slots live. `slot_row`: for live slots, the block row within the cell's row group of 8 block rows. `slot_col`: for live slots, the position within the cell's column group of 16 block columns, as in the first step.
All inputs are finite; a program needn't handle non-finite values.
Results may differ from the reference program's by a relative error of at most 0.0003.
Values sent between devices are 32-bit elements; how exact they have to be, the bound alone decides.
A program may use at most 64 MiB of HBM per device.

```python
import jax
import jax.numpy as jnp
from jax import lax

ORB = 128
NVEC = 16
PIECE = 2
ITERS = 2
GR = 8
GC = 4
NB = 64
HALF = 8
EXTRA = 24
CAP = 58


def block_pattern(key):
    base_key = jax.random.fold_in(key, 1717)
    group_rows = GC * PIECE
    group_cols = GR * PIECE
    offsets = jax.random.permutation(jax.random.fold_in(base_key, 1), NB // 2 - 1)[:HALF].astype(jnp.int32) + 1
    deltas = jnp.concatenate([jnp.zeros((1,), jnp.int32), offsets, -offsets])
    cell_rows = jnp.arange(GR, dtype=jnp.int32)
    cell_cols = jnp.arange(GC, dtype=jnp.int32)
    local_rows = jnp.arange(group_rows, dtype=jnp.int32)
    first_rows = cell_rows[:, None, None, None] * group_rows + local_rows[None, None, None, :]
    first_cols = jnp.mod(first_rows + deltas[None, None, :, None], NB)
    owners = first_cols // PIECE % GC
    matched = owners == cell_cols[None, :, None, None]
    picked = jnp.argsort(jnp.where(matched, 0, 1), axis=-1, stable=True)[..., :PIECE].astype(jnp.int32)
    base_row = cell_rows[:, None, None, None] * group_rows + picked
    base_col = jnp.mod(base_row + deltas[None, None, :, None], NB)
    base_row = base_row.reshape(GR, GC, -1)
    base_col = base_col.reshape(GR, GC, -1)
    hot_row = jax.random.randint(jax.random.fold_in(base_key, 2), (), 0, GR).astype(jnp.int32)
    hot_col = jax.random.randint(jax.random.fold_in(base_key, 3), (), 0, GC).astype(jnp.int32)
    outside = (GR - 1) * PIECE
    candidate = jnp.arange(group_rows * outside, dtype=jnp.int32)
    local_a = candidate // outside
    local_b = candidate % outside
    position = local_b + PIECE * (local_b // PIECE >= hot_row).astype(jnp.int32)
    extra_row = hot_row * group_rows + local_a
    extra_col = (position // PIECE * GC + hot_col) * PIECE + position % PIECE
    clashes = jnp.any(jnp.mod(extra_col - extra_row, NB)[:, None] == jnp.mod(deltas, NB)[None, :], axis=1)
    ranking = jax.random.permutation(jax.random.fold_in(base_key, 4), candidate.shape[0]).astype(jnp.int32)
    priority = ranking + clashes.astype(jnp.int32) * candidate.shape[0]
    chosen = jnp.argsort(priority, stable=True)[:EXTRA]
    extra_row = extra_row[chosen]
    extra_col = extra_col[chosen]
    mirror_row = extra_col // group_rows
    mirror_col = extra_row // PIECE % GC
    is_hot = (cell_rows[:, None, None] == hot_row) & (cell_cols[None, :, None] == hot_col)
    is_mirror = (mirror_row[None, None, :] == cell_rows[:, None, None]) & (mirror_col[None, None, :] == cell_cols[None, :, None])
    taken_slots = is_hot | is_mirror
    side_row = jnp.where(is_hot, extra_row[None, None, :], extra_col[None, None, :])
    side_col = jnp.where(is_hot, extra_col[None, None, :], extra_row[None, None, :])
    packing = jnp.argsort(jnp.where(taken_slots, 0, 1), axis=-1, stable=True)
    side_row = jnp.take_along_axis(side_row, packing, axis=-1)
    side_col = jnp.take_along_axis(side_col, packing, axis=-1)
    taken_slots = jnp.take_along_axis(taken_slots, packing, axis=-1)
    glob_row = jnp.concatenate([base_row, side_row], axis=-1)
    glob_col = jnp.concatenate([base_col, side_col], axis=-1)
    active = jnp.concatenate([jnp.ones(base_row.shape, bool), taken_slots], axis=-1)
    slot_ids = jnp.arange(CAP, dtype=jnp.int32)
    mixing = jax.random.randint(jax.random.fold_in(base_key, 5), (GR, GC, CAP), 0, 1 << 14).astype(jnp.int32) * CAP + slot_ids
    order_key = jnp.where(active, mixing, (1 << 14) * CAP + slot_ids)
    shuffle = jnp.argsort(order_key, axis=-1, stable=True)
    glob_row = jnp.take_along_axis(glob_row, shuffle, axis=-1)
    glob_col = jnp.take_along_axis(glob_col, shuffle, axis=-1)
    active = jnp.take_along_axis(active, shuffle, axis=-1)
    counts = jnp.sum(active.astype(jnp.int32), axis=-1).astype(jnp.int32)
    junk_rows = jax.random.randint(jax.random.fold_in(base_key, 6), (GR, GC, CAP), 0, group_rows).astype(jnp.int32)
    junk_cols = jax.random.randint(jax.random.fold_in(base_key, 7), (GR, GC, CAP), 0, group_cols).astype(jnp.int32)
    slot_row = jnp.where(active, glob_row - cell_rows[:, None, None] * group_rows, junk_rows)
    pieces_of = glob_col // PIECE
    slot_col = jnp.where(active, pieces_of // GC * PIECE + glob_col % PIECE, junk_cols)
    return (slot_row, slot_col, counts, glob_row, glob_col, active)


def draw_slot_row(key, part):
    return block_pattern(key)[0]


def draw_slot_col(key, part):
    return block_pattern(key)[1]


def draw_counts(key, part):
    return block_pattern(key)[2]


def draw_blocks(key, part):
    slot_row, slot_col, counts, glob_row, glob_col, active = block_pattern(key)
    value_key = jax.random.fold_in(key, 2929)
    sigma = (ORB * (2 * HALF + 1)) ** (-0.5)
    slot_ids = jnp.arange(CAP, dtype=jnp.int32)[None, None, :]
    cell_ids = jnp.arange(GR, dtype=jnp.int32)[:, None, None] * GC + jnp.arange(GC, dtype=jnp.int32)[None, :, None]
    lower_id = jnp.where(active, jnp.minimum(glob_row, glob_col), NB + slot_ids)
    upper_id = jnp.where(active, jnp.maximum(glob_row, glob_col), cell_ids + 0 * slot_ids)
    flipped = glob_row > glob_col
    diagonal = active & (glob_row == glob_col)

    def one_tile(lower_one, upper_one, flip_one, diag_one):
        tile_key = jax.random.fold_in(jax.random.fold_in(value_key, lower_one), upper_one)
        raw = jax.random.normal(tile_key, (ORB, ORB), jnp.float32)
        onsite = jax.random.uniform(jax.random.fold_in(tile_key, 5), (ORB,), jnp.float32, -1.0, 3.0)
        drawn = jnp.where(flip_one, raw.T, raw) * sigma
        mirrored = (raw + raw.T) * (sigma * 0.70710678) + jnp.diag(onsite)
        return jnp.where(diag_one, mirrored, drawn)

    def one_cell(item):
        return jax.vmap(one_tile)(item[0], item[1], item[2], item[3])
    cells = GR * GC
    tiles_all = lax.map(one_cell, (lower_id.reshape(cells, CAP), upper_id.reshape(cells, CAP), flipped.reshape(cells, CAP), diagonal.reshape(cells, CAP)))
    return tiles_all.reshape(GR, GC, CAP, ORB, ORB)


def level_of(stream_key, shape, split, low, largest):
    level, own = 1.0, jax.random.fold_in(stream_key, 6)
    for dim, parts in split:
        steps = jnp.exp(jax.random.uniform(jax.random.fold_in(own, dim), (parts,), jnp.float32, low / len(split), largest / len(split)))
        level = level * jnp.repeat(steps, shape[dim] // parts).reshape([-1 if axis == dim else 1 for axis in range(len(shape))])
    return level


def gaussian(own_key, dims, width, reach, shards=(), held_as=jnp.bfloat16):
    factor_of = level_of(own_key, dims, shards, -0.22, 0.18) if shards else 1.0
    entries = jax.random.normal(own_key, dims, jnp.float32) * width * factor_of
    return jnp.minimum(jnp.maximum(entries, -reach), reach).astype(held_as)


def setup_inputs(seed: int = 0) -> dict:
    seeds = jax.random.split(jax.random.key(seed), 6)
    start_block = gaussian(seeds[0], (NB, NVEC, ORB), 1.0, 6.0, ((0, 32),), jnp.float32)
    blocks = draw_blocks(jax.random.fold_in(seeds[5], 71), 0)
    slot_row = draw_slot_row(jax.random.fold_in(seeds[5], 71), 0)
    slot_col = draw_slot_col(jax.random.fold_in(seeds[5], 71), 0)
    counts = draw_counts(jax.random.fold_in(seeds[5], 71), 0)
    return dict(start_block=start_block, blocks=blocks, slot_row=slot_row, slot_col=slot_col, counts=counts)


def mean_gram(left, right):
    return jnp.einsum('bki,bli->kl', left, right, precision=lax.Precision.HIGHEST) / (NB * ORB)

def apply_operator(vectors, blocks, slot_row, slot_col, counts):
    cells = GR * GC
    tiles_all = blocks.reshape(cells, CAP, ORB, ORB)
    rows_all = slot_row.reshape(cells, CAP)
    cols_all = slot_col.reshape(cells, CAP)
    count_all = counts.reshape(cells)
    cell_ids = jnp.arange(cells, dtype=jnp.int32)

    def cell_step(running, item):
        tiles_here, rows_here, cols_here, count_here, cell_id = item
        grid_row = cell_id // GC
        grid_col = cell_id % GC
        active = jnp.arange(CAP, dtype=jnp.int32) < count_here
        global_row = (grid_row * GC * PIECE + rows_here).astype(jnp.int32)
        global_col = ((cols_here // PIECE * GC + grid_col) * PIECE + cols_here % PIECE).astype(jnp.int32)
        picked = vectors[global_col]
        product = jnp.einsum('sij,skj->ski', tiles_here, picked, precision=lax.Precision.HIGHEST)
        product = jnp.where(active[:, None, None], product, jnp.zeros_like(product))
        return (running.at[global_row].add(product), None)
    running = jnp.zeros(vectors.shape, jnp.float32)
    running, _ = lax.scan(cell_step, running, (tiles_all, rows_all, cols_all, count_all, cell_ids))
    return running

def reference(start_block, blocks, slot_row, slot_col, counts):
    identity = jnp.eye(NVEC, dtype=jnp.float32)
    factor = jnp.linalg.cholesky(mean_gram(start_block, start_block))
    inverse = jax.scipy.linalg.solve_triangular(factor, identity, lower=True)
    vectors = jnp.einsum('kl,bli->bki', inverse, start_block, precision=lax.Precision.HIGHEST)
    previous = jnp.zeros(vectors.shape, jnp.float32)
    beta_prev = jnp.zeros((NVEC, NVEC), jnp.float32)
    alpha_list = []
    beta_list = []
    for iteration in range(ITERS):
        image_block = apply_operator(vectors, blocks, slot_row, slot_col, counts)
        alpha_block = mean_gram(vectors, image_block)
        residual = image_block - jnp.einsum('lk,bli->bki', alpha_block, vectors, precision=lax.Precision.HIGHEST)
        residual = residual - jnp.einsum('kl,bli->bki', beta_prev, previous, precision=lax.Precision.HIGHEST)
        factor = jnp.linalg.cholesky(mean_gram(residual, residual))
        beta_block = factor.T
        inverse = jax.scipy.linalg.solve_triangular(factor, identity, lower=True)
        previous = vectors
        vectors = jnp.einsum('kl,bli->bki', inverse, residual, precision=lax.Precision.HIGHEST)
        beta_prev = beta_block
        alpha_list.append(alpha_block)
        beta_list.append(beta_block)
    return (jnp.stack(alpha_list), jnp.stack(beta_list), vectors)
```

```python
import functools

import jax
import jax.numpy as jnp
from jax import lax
from jax.experimental import pallas as pl
from jax.experimental.pallas import tpu as pltpu
from jax.sharding import PartitionSpec as P

HIGHEST = lax.Precision.HIGHEST
F32 = jnp.float32
BF16 = jnp.bfloat16
NN = (((1,), (0,)), ((), ()))
NT = (((1,), (1,)), ((), ()))
TN = (((0,), (0,)), ((), ()))


def dot(left, right, dims=NN):
    return lax.dot_general(left, right, dims, precision=HIGHEST, preferred_element_type=F32)


def factor(gram):
    n = gram.shape[0]
    rows = lax.broadcasted_iota(jnp.int32, (n, n), 0)
    cols = lax.broadcasted_iota(jnp.int32, (n, n), 1)
    work = jnp.concatenate([gram, (rows == cols).astype(F32)], axis=1)
    index = lax.broadcasted_iota(jnp.int32, (n, 2 * n), 0)
    spread = [jnp.broadcast_to(gram[:, j : j + 1], (n, 2 * n)) for j in range(n)]
    for j in range(n - 1):
        ratio = spread[j] / spread[j][j : j + 1]
        work = work - jnp.where(index > j, ratio, 0.0) * work[j : j + 1]
        for i in range(j + 1, n):
            spread[i] = spread[i] - ratio * spread[i][j : j + 1]
    pivots = jnp.concatenate([spread[j][j : j + 1] for j in range(n)], axis=0)
    scaled = work * (1.0 / jnp.sqrt(pivots))
    return jnp.where(rows <= cols, scaled[:, :n], 0.0), scaled[:, n:]


def pack(gram):
    quarter = gram.shape[0] // 4
    return jnp.concatenate([gram[i * quarter : (i + 1) * quarter] for i in range(4)], axis=1)


def unpack(packed):
    width = packed.shape[1] // 4
    return jnp.concatenate([packed[:, i * width : (i + 1) * width] for i in range(4)], axis=0)


def partners(size, me):
    if size & (size - 1):
        return [(lax.rem(me + d, size), lax.rem(me + size - d, size)) for d in range(size - 1, 0, -1)]
    pairs = []
    for mask in range(size - 1, 0, -1):
        other, bit = me, 1
        while bit < size:
            if mask & bit:
                other = other + bit - 2 * bit * lax.rem(me // bit, 2)
            bit *= 2
        pairs.append((other, other))
    return pairs


def kernel(
    nr, nc, group, total,
    rows_hbm, cols_hbm, counts_hbm, start_ref, blocks_ref,
    packed_ref,
    tiles, weights, gat, xs, part, scat, ybuf, gsend, grow, gcol_send, gcol,
    rows_ref, cols_ref, counts_ref,
    load_sem, row_send, row_recv, col_send, col_recv, gr_send, gr_recv, gc_send, gc_recv,
):
    me_r = lax.axis_index("row")
    me_c = lax.axis_index("col")
    capacity = tiles.shape[0]
    piece, k, orb = start_ref.shape
    local_rows = nc * piece
    row_pairs = partners(nr, me_r)
    col_pairs = partners(nc, me_c)

    loads = [
        pltpu.make_async_copy(start_ref, gat.at[0, me_r], load_sem.at[0]),
        pltpu.make_async_copy(rows_hbm, rows_ref, load_sem.at[1]),
        pltpu.make_async_copy(cols_hbm, cols_ref, load_sem.at[2]),
        pltpu.make_async_copy(counts_hbm, counts_ref, load_sem.at[3]),
        pltpu.make_async_copy(blocks_ref, tiles, load_sem.at[4]),
    ]

    barrier = pltpu.get_barrier_semaphore()
    for to, _ in row_pairs:
        pl.semaphore_signal(barrier, inc=1, device_id=(to, me_c), device_id_type=pl.DeviceIdType.MESH)
    for to, _ in col_pairs:
        pl.semaphore_signal(barrier, inc=1, device_id=(me_r, to), device_id_type=pl.DeviceIdType.MESH)
    for load in loads:
        load.start()
    loads[0].wait()
    pl.semaphore_wait(barrier, nr + nc - 2)

    def spread_row(src, dst, send, recv, step):
        copies = []
        for d, (to, _) in enumerate(row_pairs):
            copy = pltpu.make_async_remote_copy(
                src_ref=src, dst_ref=dst.at[me_r],
                send_sem=send.at[step, d], recv_sem=recv.at[step, d],
                device_id=(to, me_c), device_id_type=pl.DeviceIdType.MESH,
            )
            copy.start()
            copies.append(copy)
        return copies

    def spread_col(src, dst, send, recv, step, scatter):
        copies = []
        for d, (to, _) in enumerate(col_pairs):
            copy = pltpu.make_async_remote_copy(
                src_ref=src.at[to] if scatter else src, dst_ref=dst.at[me_c],
                send_sem=send.at[step, d], recv_sem=recv.at[step, d],
                device_id=(me_r, to), device_id_type=pl.DeviceIdType.MESH,
            )
            copy.start()
            copies.append(copy)
        return copies

    def received(copies):
        for copy in copies:
            copy.wait_recv()

    def cat(value):
        return jnp.concatenate([value[p] for p in range(piece)], axis=1)

    def mean_start(step, gram):
        gsend[step] = pack(gram) * (1.0 / total)
        return spread_row(gsend.at[step], grow.at[step], gr_send, gr_recv, step)

    def mean_row(step, copies):
        received(copies)
        grow[step, pl.ds(me_r, 1)] = gsend[step][None]
        value = grow[step, 0]
        for r in range(1, nr):
            value = value + grow[step, r]
        return value

    def mean_column(step, value):
        gcol_send[step] = value
        return spread_col(gcol_send.at[step], gcol.at[step], gc_send, gc_recv, step, False)

    def mean_end(step, copies):
        received(copies)
        gcol[step, pl.ds(me_c, 1)] = gcol_send[step][None]
        value = gcol[step, 0]
        for c in range(1, nc):
            value = value + gcol[step, c]
        return unpack(value)

    def split_vectors(step, q):
        for p in range(piece):
            value = gat[step, q, p]
            high = value.astype(BF16)
            xs[q * piece + p, :k] = high
            xs[q * piece + p, k:] = (value - high.astype(F32)).astype(BF16)

    def operate(step):
        def slot(s, accs):
            live = s < count
            col = jnp.clip(lax.select(live, cols_ref[s], 0), 0, nr * piece - 1)
            row = lax.select(live, rows_ref[s], -1)
            prod = lax.dot_general(xs[col], weights[s], NT, preferred_element_type=F32)
            prod = prod[:k, :orb] + prod[:k, orb:] + prod[k:, :orb]
            zero = jnp.zeros_like(prod)
            return [acc + lax.select(row == r, prod, zero) for r, acc in enumerate(accs)]

        accs = [jnp.zeros((k, orb), F32)] * local_rows
        if capacity == group:
            for s in range(capacity):
                accs = slot(s, accs)
        else:
            def chunk(g, accs):
                for t in range(group):
                    accs = slot(g * group + t, accs)
                return accs

            accs = lax.fori_loop(0, capacity // group, chunk, accs)
        for r in range(local_rows):
            part[step, r // piece, r % piece] = accs[r]
        return spread_col(part.at[step], scat.at[step], col_send, col_recv, step, True)

    def reduced(step, copies):
        received(copies)
        own = part[step, me_c]
        for _, other in col_pairs:
            own = own + scat[step, other]
        return own

    pending = []
    first = spread_row(gat.at[0, me_r], gat.at[0], row_send, row_recv, 0)
    pending += first
    for load in loads[1:]:
        load.wait()
    count = counts_ref[0, 0]

    def split_tile(s, carry):
        tile = tiles[s]
        high = tile.astype(BF16)
        weights[s, :orb] = high
        weights[s, orb:] = (tile - high.astype(F32)).astype(BF16)
        return carry

    lax.fori_loop(0, capacity, split_tile, 0, unroll=2)
    split_vectors(0, me_r)
    for copy, (_, other) in list(zip(first, row_pairs))[::-1]:
        copy.wait_recv()
        split_vectors(0, other)
    scatter0 = operate(0)
    pending += scatter0
    s_all = jnp.concatenate([gat[0, r, p] for r in range(nr) for p in range(piece)], axis=1)
    ss = dot(s_all, s_all, NT)
    ss = jnp.concatenate([ss, ss], axis=1)
    middle_s = mean_column(0, pack(jnp.concatenate([ss, ss], axis=0)) * (1.0 / total))
    pending += middle_s
    y_raw = reduced(0, scatter0)
    ybuf[...] = y_raw
    gat[1, pl.ds(me_r, 1)] = y_raw[None]
    second = spread_row(ybuf, gat.at[1], row_send, row_recv, 1)
    pending += second
    _, inv0 = factor(mean_end(0, middle_s)[:k, :k])
    v1 = dot(inv0, cat(gat[0, me_r]))
    hv1 = dot(inv0, cat(y_raw))

    def gram_of(q, left, right):
        both = jnp.concatenate([left, right], axis=0)
        return dot(both, both, NT)

    split_vectors(1, me_r)
    both = gram_of(me_r, v1, hv1)
    for copy, (_, other) in list(zip(second, row_pairs))[::-1]:
        left = dot(inv0, cat(gat[0, other]))
        copy.wait_recv()
        split_vectors(1, other)
        both = both + gram_of(other, left, dot(inv0, cat(gat[1, other])))
    middle0 = mean_column(1, pack(both) * (1.0 / total))
    pending += middle0
    scatter1 = operate(1)
    pending += scatter1
    gram = mean_end(1, middle0)
    q1, alpha1, yy1 = gram[:k, :k], gram[:k, k:], gram[k:, k:]
    beta1, inv1 = factor(yy1 - dot(alpha1, alpha1, TN) - dot(alpha1, alpha1 - dot(q1, alpha1), TN))
    v2 = dot(inv1, hv1 - dot(alpha1, v1, TN))
    known = dot(beta1, v1)
    shift = dot(dot(inv1, alpha1, NT), hv1)
    lead = dot(inv1, inv0)
    y2 = dot(lead, cat(reduced(1, scatter1))) - shift
    w2 = y2 - known
    both = jnp.concatenate([v2, w2], axis=0)
    grams = dot(both, jnp.concatenate([both, y2], axis=0), NT)
    top = grams[:k, : 2 * k]
    low = jnp.concatenate([grams[:k, 2 * k :], grams[k:, k : 2 * k]], axis=1)
    mean1 = mean_start(0, jnp.concatenate([top, low], axis=0))
    pending += mean1
    middle1 = mean_column(2, mean_row(0, mean1))
    pending += middle1
    gram = mean_end(2, middle1)
    qq, pw, alpha2, ww = gram[:k, :k], gram[:k, k:], gram[k:, :k], gram[k:, k:]
    rest = pw - dot(qq, alpha2)
    beta2, inv2 = factor(ww - dot(pw, alpha2, TN) - dot(alpha2, rest, TN))
    out = dot(inv2, w2 - dot(alpha2, v2, TN))
    for p in range(piece):
        packed_ref[p, :, :orb] = out[:, p * orb : (p + 1) * orb]
    packed_ref[piece, :, : 4 * k] = jnp.concatenate([alpha1, alpha2, beta1, beta2], axis=1)
    for copy in pending:
        copy.wait_send()


def finish(packed_ref, alphas_ref, betas_ref, next_ref):
    piece, k, _ = next_ref.shape
    small = packed_ref[piece]
    for step in range(2):
        alphas_ref[step] = small[:, step * k : (step + 1) * k]
        betas_ref[step] = small[:, (2 + step) * k : (3 + step) * k]
    next_ref[...] = packed_ref[:piece]


def on_device(nr, nc, start_block, blocks, slot_row, slot_col, counts):
    capacity = blocks.shape[2]
    orb = blocks.shape[3]
    piece, k, _ = start_block.shape
    local_rows = nc * piece
    total = float(piece * nr * nc * orb)
    group = max(g for g in range(1, 65) if capacity % g == 0)
    vmem = pl.BlockSpec(memory_space=pltpu.VMEM)
    dma = pltpu.SemaphoreType.DMA
    width = 4 * 2 * k
    height = 2 * k // 4
    packed = pl.pallas_call(
        functools.partial(kernel, nr, nc, group, total),
        out_shape=pltpu.VMEM((piece + 1, k, orb), F32),
        in_specs=[pl.BlockSpec(memory_space=pltpu.HBM)] * 5,
        out_specs=vmem,
        scratch_shapes=[
            pltpu.VMEM((capacity, orb, orb), F32),
            pltpu.VMEM((capacity, 2 * orb, orb), BF16),
            pltpu.VMEM((2, nr, piece, k, orb), F32),
            pltpu.VMEM((nr * piece, 2 * k, orb), BF16),
            pltpu.VMEM((2, nc, piece, k, orb), F32),
            pltpu.VMEM((2, nc, piece, k, orb), F32),
            pltpu.VMEM((piece, k, orb), F32),
            pltpu.VMEM((1, height, width), F32),
            pltpu.VMEM((1, nr, height, width), F32),
            pltpu.VMEM((3, height, width), F32),
            pltpu.VMEM((3, nc, height, width), F32),
            pltpu.SMEM((capacity,), jnp.int32),
            pltpu.SMEM((capacity,), jnp.int32),
            pltpu.SMEM((1, 1), jnp.int32),
            dma((5,)),
            dma((2, nr)), dma((2, nr)),
            dma((2, nc)), dma((2, nc)),
            dma((1, nr)), dma((1, nr)),
            dma((3, nc)), dma((3, nc)),
        ],
        compiler_params=pltpu.CompilerParams(
            collective_id=0, has_side_effects=True, vmem_limit_bytes=56 << 20
        ),
    )(slot_row[0, 0], slot_col[0, 0], counts, start_block, blocks[0, 0])
    return pl.pallas_call(
        finish,
        out_shape=(
            jax.ShapeDtypeStruct((2, k, k), F32),
            jax.ShapeDtypeStruct((2, k, k), F32),
            jax.ShapeDtypeStruct((piece, k, orb), F32),
        ),
        in_specs=[vmem],
        out_specs=(vmem, vmem, vmem),
    )(pltpu.with_memory_space_constraint(packed, pltpu.VMEM))


def solution(mesh):
    placed = (
        P(("row", "col"), None, None),
        P("row", "col", None, None, None),
        P("row", "col", None),
        P("row", "col", None),
        P("row", "col"),
    )
    return jax.shard_map(
        functools.partial(on_device, mesh.shape["row"], mesh.shape["col"]),
        mesh=mesh,
        in_specs=placed,
        out_specs=(P(), P(), P(("row", "col"), None, None)),
        check_vma=False,
    )
```

```python
import functools

import jax
import jax.numpy as jnp
from jax import lax
from jax.experimental import pallas as pl
from jax.experimental.pallas import tpu as pltpu
from jax.sharding import PartitionSpec as P

HIGHEST = lax.Precision.HIGHEST
F32 = jnp.float32
BF16 = jnp.bfloat16
NN = (((1,), (0,)), ((), ()))
NT = (((1,), (1,)), ((), ()))
TN = (((0,), (0,)), ((), ()))


def dot(left, right, dims=NN):
    return lax.dot_general(left, right, dims, precision=HIGHEST, preferred_element_type=F32)


def factor(gram):
    n = gram.shape[0]
    rows = lax.broadcasted_iota(jnp.int32, (n, n), 0)
    cols = lax.broadcasted_iota(jnp.int32, (n, n), 1)
    work = jnp.concatenate([gram, (rows == cols).astype(F32)], axis=1)
    index = lax.broadcasted_iota(jnp.int32, (n, 2 * n), 0)
    spread = [jnp.broadcast_to(gram[:, j : j + 1], (n, 2 * n)) for j in range(n)]
    for j in range(n - 1):
        ratio = spread[j] / spread[j][j : j + 1]
        work = work - jnp.where(index > j, ratio, 0.0) * work[j : j + 1]
        for i in range(j + 1, n):
            spread[i] = spread[i] - ratio * spread[i][j : j + 1]
    pivots = jnp.concatenate([spread[j][j : j + 1] for j in range(n)], axis=0)
    scaled = work * (1.0 / jnp.sqrt(pivots))
    return jnp.where(rows <= cols, scaled[:, :n], 0.0), scaled[:, n:]


def pack(blocks):
    half = blocks[0].shape[0] // 2
    return jnp.concatenate([block[h * half : (h + 1) * half] for block in blocks for h in range(2)], axis=1)


def unpack(packed):
    width = packed.shape[1] // 8
    parts = [packed[:, i * width : (i + 1) * width] for i in range(8)]
    return [jnp.concatenate(parts[2 * i : 2 * i + 2], axis=0) for i in range(4)]


def partners(size, me):
    if size & (size - 1):
        return [(lax.rem(me + d, size), lax.rem(me + size - d, size)) for d in range(size - 1, 0, -1)]
    pairs = []
    for mask in range(size - 1, 0, -1):
        other, bit = me, 1
        while bit < size:
            if mask & bit:
                other = other + bit - 2 * bit * lax.rem(me // bit, 2)
            bit *= 2
        pairs.append((other, other))
    return pairs


def others(size, me):
    upper = 2 * me // size
    order = []
    for j in range(size - 1):
        down = size - 1 - j - (me + j) // (size - 1)
        up = j + 1 - (me + size - 1 - j) // size
        order.append(down + upper * (up - down))
    return order


def kernel(
    nr, nc, group, total,
    rows_hbm, cols_hbm, counts_hbm, start_ref, blocks_ref,
    packed_ref,
    tiles, weights, gat, vbuf, xs, part, scat, ybuf, gsend, grow, gcol_send, gcol,
    rows_ref, cols_ref, counts_ref,
    load_sem, row_send, row_recv, piece_recv, col_send, col_recv, gr_send, gr_recv, gc_send, gc_recv,
):
    me_r = lax.axis_index("row")
    me_c = lax.axis_index("col")
    capacity = tiles.shape[0]
    piece, k, orb = start_ref.shape
    local_rows = nc * piece
    row_pairs = partners(nr, me_r)
    col_pairs = partners(nc, me_c)

    loads = [
        pltpu.make_async_copy(start_ref, gat.at[0, me_r], load_sem.at[0]),
        pltpu.make_async_copy(rows_hbm, rows_ref, load_sem.at[1]),
        pltpu.make_async_copy(cols_hbm, cols_ref, load_sem.at[2]),
        pltpu.make_async_copy(counts_hbm, counts_ref, load_sem.at[3]),
        pltpu.make_async_copy(blocks_ref, tiles, load_sem.at[4]),
    ]

    barrier = pltpu.get_barrier_semaphore()
    for to, _ in row_pairs:
        pl.semaphore_signal(barrier, inc=1, device_id=(to, me_c), device_id_type=pl.DeviceIdType.MESH)
    for to, _ in col_pairs:
        pl.semaphore_signal(barrier, inc=1, device_id=(me_r, to), device_id_type=pl.DeviceIdType.MESH)
    for load in loads:
        load.start()
    loads[0].wait()
    pl.semaphore_wait(barrier, nr + nc - 2)

    pending = []
    waits = list(range(nr - 2, nr // 2 - 1, -1)) + list(range(nr // 2))

    def spread_row(src, dst, send, recv, step, peers, apart=False):
        copies = []
        for d, to in enumerate(peers):
            copy = pltpu.make_async_remote_copy(
                src_ref=src, dst_ref=dst.at[me_r],
                send_sem=send.at[step], recv_sem=recv.at[d] if apart else recv.at[step],
                device_id=(to, me_c), device_id_type=pl.DeviceIdType.MESH,
            )
            copy.start()
            copies.append(copy)
        pending.append((dst.at[pl.ds(0, nr - 1)], send.at[step]))
        return copies if apart else (dst.at[pl.ds(0, nr - 1)], recv.at[step])

    def spread_col(src, dst, send, recv, step, scatter):
        for to, _ in col_pairs:
            copy = pltpu.make_async_remote_copy(
                src_ref=src.at[to] if scatter else src, dst_ref=dst.at[me_c],
                send_sem=send.at[step], recv_sem=recv.at[step],
                device_id=(me_r, to), device_id_type=pl.DeviceIdType.MESH,
            )
            copy.start()
        pending.append((dst.at[pl.ds(0, nc - 1)], send.at[step]))
        return dst.at[pl.ds(0, nc - 1)], recv.at[step]

    def settled(like, sem):
        pltpu.make_async_copy(like, like, sem).wait()

    def cat(value):
        return jnp.concatenate([value[p] for p in range(piece)], axis=1)

    def mean_start(step, blocks):
        gsend[step] = pack(blocks) * (1.0 / total)
        return spread_row(gsend.at[step], grow.at[step], gr_send, gr_recv, step, [to for to, _ in row_pairs])

    def mean_row(step, copies):
        settled(*copies)
        grow[step, pl.ds(me_r, 1)] = gsend[step][None]
        value = grow[step, 0]
        for r in range(1, nr):
            value = value + grow[step, r]
        return value

    def mean_column(step, value):
        gcol_send[step] = value
        return spread_col(gcol_send.at[step], gcol.at[step], gc_send, gc_recv, step, False)

    def mean_end(step, copies):
        settled(*copies)
        gcol[step, pl.ds(me_c, 1)] = gcol_send[step][None]
        value = gcol[step, 0]
        for c in range(1, nc):
            value = value + gcol[step, c]
        return unpack(value)

    def split_vectors(step, q):
        for p in range(piece):
            value = gat[step, q, p]
            high = value.astype(BF16)
            xs[q * piece + p, :k] = high
            xs[q * piece + p, k:] = (value - high.astype(F32)).astype(BF16)

    def operate(step):
        def slot(s, accs):
            live = s < count
            col = jnp.clip(lax.select(live, cols_ref[s], 0), 0, nr * piece - 1)
            row = lax.select(live, rows_ref[s], -1)
            prod = lax.dot_general(xs[col], weights[s], NN, preferred_element_type=F32)
            prod = prod[:k, :orb] + prod[:k, orb:] + prod[k:, :orb]
            zero = jnp.zeros_like(prod)
            return [acc + lax.select(row == r, prod, zero) for r, acc in enumerate(accs)]

        accs = [jnp.zeros((k, orb), F32)] * local_rows
        if capacity == group:
            for s in range(capacity):
                accs = slot(s, accs)
        else:
            def chunk(g, accs):
                for t in range(group):
                    accs = slot(g * group + t, accs)
                return accs

            accs = lax.fori_loop(0, capacity // group, chunk, accs)
        for r in range(local_rows):
            part[step, r // piece, r % piece] = accs[r]
        return spread_col(part.at[step], scat.at[step], col_send, col_recv, step, True)

    def reduced(step, copies):
        settled(*copies)
        own = part[step, me_c]
        for _, other in col_pairs:
            own = own + scat[step, other]
        return own

    first = spread_row(gat.at[0, me_r], gat.at[0], row_send, row_recv, 0, others(nr, me_r))
    for load in loads[1:]:
        load.wait()
    count = counts_ref[0, 0]

    def split_tile(s, carry):
        tile = tiles[s].T
        high = tile.astype(BF16)
        weights[s, :, :orb] = high
        weights[s, :, orb:] = (tile - high.astype(F32)).astype(BF16)
        return carry

    lax.fori_loop(0, capacity, split_tile, 0, unroll=2)
    split_vectors(0, me_r)
    settled(*first)
    for _, other in row_pairs:
        split_vectors(0, other)
    scatter0 = operate(0)
    s_all = jnp.concatenate([gat[0, r, p] for r in range(nr) for p in range(piece)], axis=1)
    ss = dot(s_all, s_all, NT)
    middle_s = mean_column(0, pack([ss] * 4) * (1.0 / total))
    y_raw = reduced(0, scatter0)
    ybuf[...] = y_raw
    gat[1, pl.ds(me_r, 1)] = y_raw[None]
    second = spread_row(ybuf, gat.at[1], row_send, piece_recv, 1, [to for to, _ in row_pairs], True)
    _, inv0 = factor(mean_end(0, middle_s)[0])
    hv1 = dot(inv0, cat(y_raw))
    v_all = dot(inv0, s_all)
    for r in range(nr):
        vbuf[r] = v_all[:, r * piece * orb : (r + 1) * piece * orb]
    v1 = vbuf[me_r]

    def gram_of(left, right):
        both = jnp.concatenate([left, right], axis=0)
        return dot(both, both, NT)

    split_vectors(1, me_r)
    both = gram_of(v1, hv1)
    for d in waits:
        other = row_pairs[d][1]
        second[d].wait_recv()
        split_vectors(1, other)
        both = both + gram_of(vbuf[other], dot(inv0, cat(gat[1, other])))
    middle0 = mean_column(1, pack([both[:k, :k], both[:k, k:], both[k:, k:], both[k:, k:]]) * (1.0 / total))
    scatter1 = operate(1)
    q1, alpha1, yy1, _ = mean_end(1, middle0)
    w1 = hv1 - dot(alpha1, v1, TN)
    drift = dot(alpha1, hv1, TN)
    beta1, inv1 = factor(yy1 - dot(alpha1, alpha1 + (alpha1 - dot(q1, alpha1)), TN))
    v2 = dot(inv1, w1)
    known = dot(beta1, v1)
    shift = dot(inv1, drift)
    lead = dot(inv1, inv0)
    y2 = dot(lead, cat(reduced(1, scatter1))) - shift
    w2 = y2 - known
    both = jnp.concatenate([v2, w2], axis=0)
    grams = dot(both, jnp.concatenate([both, y2], axis=0), NT)
    mean1 = mean_start(0, [grams[:k, :k], grams[:k, k : 2 * k], grams[:k, 2 * k :], grams[k:, k : 2 * k]])
    middle1 = mean_column(2, mean_row(0, mean1))
    qq, pw, alpha2, ww = mean_end(2, middle1)
    rest = pw - dot(qq, alpha2)
    beta2, inv2 = factor(ww - dot(pw, alpha2, TN) - dot(alpha2, rest, TN))
    out = dot(inv2, w2 - dot(alpha2, v2, TN))
    for p in range(piece):
        packed_ref[p, :, :orb] = out[:, p * orb : (p + 1) * orb]
    packed_ref[piece, :, : 4 * k] = jnp.concatenate([alpha1, alpha2, beta1, beta2], axis=1)
    for like, sem in pending:
        settled(like, sem)


def finish(packed_ref, alphas_ref, betas_ref, next_ref):
    piece, k, _ = next_ref.shape
    small = packed_ref[piece]
    for step in range(2):
        alphas_ref[step] = small[:, step * k : (step + 1) * k]
        betas_ref[step] = small[:, (2 + step) * k : (3 + step) * k]
    next_ref[...] = packed_ref[:piece]


def on_device(nr, nc, start_block, blocks, slot_row, slot_col, counts):
    capacity = blocks.shape[2]
    orb = blocks.shape[3]
    piece, k, _ = start_block.shape
    local_rows = nc * piece
    total = float(piece * nr * nc * orb)
    group = max(g for g in range(1, 65) if capacity % g == 0)
    vmem = pl.BlockSpec(memory_space=pltpu.VMEM)
    dma = pltpu.SemaphoreType.DMA
    width = 4 * 2 * k
    height = k // 2
    packed = pl.pallas_call(
        functools.partial(kernel, nr, nc, group, total),
        out_shape=pltpu.VMEM((piece + 1, k, orb), F32),
        in_specs=[pl.BlockSpec(memory_space=pltpu.HBM)] * 5,
        out_specs=vmem,
        scratch_shapes=[
            pltpu.VMEM((capacity, orb, orb), F32),
            pltpu.VMEM((capacity, orb, 2 * orb), BF16),
            pltpu.VMEM((2, nr, piece, k, orb), F32),
            pltpu.VMEM((nr, k, piece * orb), F32),
            pltpu.VMEM((nr * piece, 2 * k, orb), BF16),
            pltpu.VMEM((2, nc, piece, k, orb), F32),
            pltpu.VMEM((2, nc, piece, k, orb), F32),
            pltpu.VMEM((piece, k, orb), F32),
            pltpu.VMEM((1, height, width), F32),
            pltpu.VMEM((1, nr, height, width), F32),
            pltpu.VMEM((3, height, width), F32),
            pltpu.VMEM((3, nc, height, width), F32),
            pltpu.SMEM((capacity,), jnp.int32),
            pltpu.SMEM((capacity,), jnp.int32),
            pltpu.SMEM((1, 1), jnp.int32),
            dma((5,)),
            dma((2,)), dma((1,)), dma((nr - 1,)),
            dma((2,)), dma((2,)),
            dma((1,)), dma((1,)),
            dma((3,)), dma((3,)),
        ],
        compiler_params=pltpu.CompilerParams(
            collective_id=0, has_side_effects=True, vmem_limit_bytes=56 << 20
        ),
    )(slot_row[0, 0], slot_col[0, 0], counts, start_block, blocks[0, 0])
    return pl.pallas_call(
        finish,
        out_shape=(
            jax.ShapeDtypeStruct((2, k, k), F32),
            jax.ShapeDtypeStruct((2, k, k), F32),
            jax.ShapeDtypeStruct((piece, k, orb), F32),
        ),
        in_specs=[vmem],
        out_specs=(vmem, vmem, vmem),
    )(pltpu.with_memory_space_constraint(packed, pltpu.VMEM))


def solution(mesh):
    placed = (
        P(("row", "col"), None, None),
        P("row", "col", None, None, None),
        P("row", "col", None),
        P("row", "col", None),
        P("row", "col"),
    )
    return jax.shard_map(
        functools.partial(on_device, mesh.shape["row"], mesh.shape["col"]),
        mesh=mesh,
        in_specs=placed,
        out_specs=(P(), P(), P(("row", "col"), None, None)),
        check_vma=False,
    )
```

```python
import functools

import jax
import jax.numpy as jnp
from jax import lax
from jax.experimental import pallas as pl
from jax.experimental.pallas import tpu as pltpu
from jax.sharding import PartitionSpec as P

HIGHEST = lax.Precision.HIGHEST
F32 = jnp.float32
BF16 = jnp.bfloat16
NN = (((1,), (0,)), ((), ()))
NT = (((1,), (1,)), ((), ()))
TN = (((0,), (0,)), ((), ()))


def dot(left, right, dims=NN):
    return lax.dot_general(left, right, dims, precision=HIGHEST, preferred_element_type=F32)


def small(left, right):
    n = left.shape[0]
    terms = [jnp.broadcast_to(left[:, j : j + 1], (n, n)) * right[j : j + 1] for j in range(n)]
    while len(terms) > 1:
        terms = [terms[i] + terms[i + 1] for i in range(0, len(terms) - 1, 2)] + terms[len(terms) - len(terms) % 2 :]
    return terms[0]


def factor(gram):
    n = gram.shape[0]
    rows = lax.broadcasted_iota(jnp.int32, (n, n), 0)
    cols = lax.broadcasted_iota(jnp.int32, (n, n), 1)
    work = jnp.concatenate([gram, (rows == cols).astype(F32)], axis=1)
    index = lax.broadcasted_iota(jnp.int32, (n, 2 * n), 0)
    spread = [jnp.broadcast_to(gram[:, j : j + 1], (n, 2 * n)) for j in range(n)]
    for j in range(n - 1):
        ratio = spread[j] / spread[j][j : j + 1]
        work = work - jnp.where(index > j, ratio, 0.0) * work[j : j + 1]
        for i in range(j + 1, n):
            spread[i] = spread[i] - ratio * spread[i][j : j + 1]
    pivots = jnp.concatenate([spread[j][j : j + 1] for j in range(n)], axis=0)
    scaled = work * (1.0 / jnp.sqrt(pivots))
    return jnp.where(rows <= cols, scaled[:, :n], 0.0), scaled[:, n:]


def pack(blocks):
    half = blocks[0].shape[0] // 2
    return jnp.concatenate([block[h * half : (h + 1) * half] for block in blocks for h in range(2)], axis=1)


def unpack(packed):
    width = packed.shape[1] // 8
    parts = [packed[:, i * width : (i + 1) * width] for i in range(8)]
    return [jnp.concatenate(parts[2 * i : 2 * i + 2], axis=0) for i in range(4)]


def partners(size, me):
    if size & (size - 1):
        return [(lax.rem(me + d, size), lax.rem(me + size - d, size)) for d in range(size - 1, 0, -1)]
    pairs = []
    for mask in range(size - 1, 0, -1):
        other, bit = me, 1
        while bit < size:
            if mask & bit:
                other = other + bit - 2 * bit * lax.rem(me // bit, 2)
            bit *= 2
        pairs.append((other, other))
    return pairs


def others(size, me):
    upper = 2 * me // size
    order = []
    for j in range(size - 1):
        down = size - 1 - j - (me + j) // (size - 1)
        up = j + 1 - (me + size - 1 - j) // size
        order.append(down + upper * (up - down))
    return order


def kernel(
    nr, nc, group, total,
    rows_hbm, cols_hbm, counts_hbm, start_ref, blocks_ref,
    packed_ref,
    tiles, weights, gat, vbuf, xs, part, scat, ybuf, gsend, grow, gcol_send, gcol,
    rows_ref, cols_ref, counts_ref,
    load_sem, row_send, row_recv, piece_recv, col_send, col_recv, gr_send, gr_recv, gc_send, gc_recv,
):
    me_r = lax.axis_index("row")
    me_c = lax.axis_index("col")
    capacity = tiles.shape[0]
    piece, k, orb = start_ref.shape
    local_rows = nc * piece
    row_pairs = partners(nr, me_r)
    col_pairs = partners(nc, me_c)

    loads = [
        pltpu.make_async_copy(start_ref, gat.at[0, me_r], load_sem.at[0]),
        pltpu.make_async_copy(rows_hbm, rows_ref, load_sem.at[1]),
        pltpu.make_async_copy(cols_hbm, cols_ref, load_sem.at[2]),
        pltpu.make_async_copy(counts_hbm, counts_ref, load_sem.at[3]),
        pltpu.make_async_copy(blocks_ref, tiles, load_sem.at[4]),
    ]

    barrier = pltpu.get_barrier_semaphore()
    for to, _ in row_pairs:
        pl.semaphore_signal(barrier, inc=1, device_id=(to, me_c), device_id_type=pl.DeviceIdType.MESH)
    for to, _ in col_pairs:
        pl.semaphore_signal(barrier, inc=1, device_id=(me_r, to), device_id_type=pl.DeviceIdType.MESH)
    for load in loads:
        load.start()
    loads[0].wait()
    pl.semaphore_wait(barrier, nr + nc - 2)

    pending = []
    waits = list(range(nr - 2, nr // 2 - 1, -1)) + list(range(nr // 2))

    def spread_row(src, dst, send, recv, step, peers, apart=False):
        copies = []
        for d, to in enumerate(peers):
            copy = pltpu.make_async_remote_copy(
                src_ref=src, dst_ref=dst.at[me_r],
                send_sem=send.at[step], recv_sem=recv.at[d] if apart else recv.at[step],
                device_id=(to, me_c), device_id_type=pl.DeviceIdType.MESH,
            )
            copy.start()
            copies.append(copy)
        pending.append((dst.at[pl.ds(0, nr - 1)], send.at[step]))
        return copies if apart else (dst.at[pl.ds(0, nr - 1)], recv.at[step])

    def spread_col(src, dst, send, recv, step, scatter):
        for to, _ in col_pairs:
            copy = pltpu.make_async_remote_copy(
                src_ref=src.at[to] if scatter else src, dst_ref=dst.at[me_c],
                send_sem=send.at[step], recv_sem=recv.at[step],
                device_id=(me_r, to), device_id_type=pl.DeviceIdType.MESH,
            )
            copy.start()
        pending.append((dst.at[pl.ds(0, nc - 1)], send.at[step]))
        return dst.at[pl.ds(0, nc - 1)], recv.at[step]

    def settled(like, sem):
        pltpu.make_async_copy(like, like, sem).wait()

    def cat(value):
        return jnp.concatenate([value[p] for p in range(piece)], axis=1)

    def mean_start(step, blocks):
        gsend[step] = pack(blocks) * (1.0 / total)
        return spread_row(gsend.at[step], grow.at[step], gr_send, gr_recv, step, [to for to, _ in row_pairs])

    def mean_row(step, copies):
        settled(*copies)
        grow[step, pl.ds(me_r, 1)] = gsend[step][None]
        value = grow[step, 0]
        for r in range(1, nr):
            value = value + grow[step, r]
        return value

    def mean_column(step, value):
        gcol_send[step] = value
        return spread_col(gcol_send.at[step], gcol.at[step], gc_send, gc_recv, step, False)

    def mean_end(step, copies):
        settled(*copies)
        gcol[step, pl.ds(me_c, 1)] = gcol_send[step][None]
        value = gcol[step, 0]
        for c in range(1, nc):
            value = value + gcol[step, c]
        return unpack(value)

    def split_vectors(step, q):
        for p in range(piece):
            value = gat[step, q, p]
            high = value.astype(BF16)
            xs[q * piece + p, :k] = high
            xs[q * piece + p, k:] = (value - high.astype(F32)).astype(BF16)

    def operate(step):
        def slot(s, accs):
            live = s < count
            col = jnp.clip(lax.select(live, cols_ref[s], 0), 0, nr * piece - 1)
            row = lax.select(live, rows_ref[s], -1)
            prod = lax.dot_general(xs[col], weights[s], NN, preferred_element_type=F32)
            prod = prod[:k, :orb] + prod[:k, orb:] + prod[k:, :orb]
            zero = jnp.zeros_like(prod)
            return [acc + lax.select(row == r, prod, zero) for r, acc in enumerate(accs)]

        accs = [jnp.zeros((k, orb), F32)] * local_rows
        if capacity == group:
            for s in range(capacity):
                accs = slot(s, accs)
        else:
            def chunk(g, accs):
                for t in range(group):
                    accs = slot(g * group + t, accs)
                return accs

            accs = lax.fori_loop(0, capacity // group, chunk, accs)
        for r in range(local_rows):
            part[step, r // piece, r % piece] = accs[r]
        return spread_col(part.at[step], scat.at[step], col_send, col_recv, step, True)

    def reduced(step, copies):
        settled(*copies)
        own = part[step, me_c]
        for _, other in col_pairs:
            own = own + scat[step, other]
        return own

    first = spread_row(gat.at[0, me_r], gat.at[0], row_send, row_recv, 0, others(nr, me_r))
    for load in loads[1:]:
        load.wait()
    count = counts_ref[0, 0]

    def split_tile(s, carry):
        tile = tiles[s].T
        high = tile.astype(BF16)
        weights[s, :, :orb] = high
        weights[s, :, orb:] = (tile - high.astype(F32)).astype(BF16)
        return carry

    lax.fori_loop(0, capacity, split_tile, 0, unroll=2)
    split_vectors(0, me_r)
    settled(*first)
    for _, other in row_pairs:
        split_vectors(0, other)
    scatter0 = operate(0)
    s_all = jnp.concatenate([gat[0, r, p] for r in range(nr) for p in range(piece)], axis=1)
    ss = dot(s_all, s_all, NT)
    middle_s = mean_column(0, pack([ss] * 4) * (1.0 / total))
    y_raw = reduced(0, scatter0)
    ybuf[...] = y_raw
    gat[1, pl.ds(me_r, 1)] = y_raw[None]
    second = spread_row(ybuf, gat.at[1], row_send, piece_recv, 1, [to for to, _ in row_pairs], True)
    _, inv0 = factor(mean_end(0, middle_s)[0])
    hv1 = dot(inv0, cat(y_raw))
    v_all = dot(inv0, s_all)
    for r in range(nr):
        vbuf[r] = v_all[:, r * piece * orb : (r + 1) * piece * orb]
    v1 = vbuf[me_r]

    def gram_of(left, right):
        both = jnp.concatenate([left, right], axis=0)
        return dot(both, both, NT)

    split_vectors(1, me_r)
    both = gram_of(v1, hv1)
    for d in waits:
        other = row_pairs[d][1]
        second[d].wait_recv()
        split_vectors(1, other)
        both = both + gram_of(vbuf[other], dot(inv0, cat(gat[1, other])))
    middle0 = mean_column(1, pack([both[:k, :k], both[:k, k:], both[k:, k:], both[k:, k:]]) * (1.0 / total))
    scatter1 = operate(1)
    q1, alpha1, yy1, _ = mean_end(1, middle0)
    turned1 = alpha1.T
    beta1, inv1 = factor(yy1 - small(turned1, alpha1 + (alpha1 - small(q1, alpha1))))
    w1 = hv1 - dot(turned1, v1)
    drift = dot(turned1, hv1)
    v2 = dot(inv1, w1)
    known = dot(beta1, v1)
    shift = dot(inv1, drift)
    lead = small(inv1, inv0)
    y2 = dot(lead, cat(reduced(1, scatter1))) - shift
    w2 = y2 - known
    both = jnp.concatenate([v2, w2], axis=0)
    grams = dot(both, jnp.concatenate([both, y2], axis=0), NT)
    mean1 = mean_start(0, [grams[:k, :k], grams[:k, k : 2 * k], grams[:k, 2 * k :], grams[k:, k : 2 * k]])
    middle1 = mean_column(2, mean_row(0, mean1))
    qq, pw, alpha2, ww = mean_end(2, middle1)
    turned2 = alpha2.T
    rest = pw - small(qq, alpha2)
    beta2, inv2 = factor(ww - small(pw.T, alpha2) - small(turned2, rest))
    out = dot(inv2, w2 - dot(turned2, v2))
    for p in range(piece):
        packed_ref[p, :, :orb] = out[:, p * orb : (p + 1) * orb]
    packed_ref[piece, :, : 4 * k] = jnp.concatenate([alpha1, alpha2, beta1, beta2], axis=1)
    for like, sem in pending:
        settled(like, sem)


def finish(packed_ref, alphas_ref, betas_ref, next_ref):
    piece, k, _ = next_ref.shape
    small = packed_ref[piece]
    for step in range(2):
        alphas_ref[step] = small[:, step * k : (step + 1) * k]
        betas_ref[step] = small[:, (2 + step) * k : (3 + step) * k]
    next_ref[...] = packed_ref[:piece]


def on_device(nr, nc, start_block, blocks, slot_row, slot_col, counts):
    capacity = blocks.shape[2]
    orb = blocks.shape[3]
    piece, k, _ = start_block.shape
    local_rows = nc * piece
    total = float(piece * nr * nc * orb)
    group = max(g for g in range(1, 65) if capacity % g == 0)
    vmem = pl.BlockSpec(memory_space=pltpu.VMEM)
    dma = pltpu.SemaphoreType.DMA
    width = 4 * 2 * k
    height = k // 2
    packed = pl.pallas_call(
        functools.partial(kernel, nr, nc, group, total),
        out_shape=pltpu.VMEM((piece + 1, k, orb), F32),
        in_specs=[pl.BlockSpec(memory_space=pltpu.HBM)] * 5,
        out_specs=vmem,
        scratch_shapes=[
            pltpu.VMEM((capacity, orb, orb), F32),
            pltpu.VMEM((capacity, orb, 2 * orb), BF16),
            pltpu.VMEM((2, nr, piece, k, orb), F32),
            pltpu.VMEM((nr, k, piece * orb), F32),
            pltpu.VMEM((nr * piece, 2 * k, orb), BF16),
            pltpu.VMEM((2, nc, piece, k, orb), F32),
            pltpu.VMEM((2, nc, piece, k, orb), F32),
            pltpu.VMEM((piece, k, orb), F32),
            pltpu.VMEM((1, height, width), F32),
            pltpu.VMEM((1, nr, height, width), F32),
            pltpu.VMEM((3, height, width), F32),
            pltpu.VMEM((3, nc, height, width), F32),
            pltpu.SMEM((capacity,), jnp.int32),
            pltpu.SMEM((capacity,), jnp.int32),
            pltpu.SMEM((1, 1), jnp.int32),
            dma((5,)),
            dma((2,)), dma((1,)), dma((nr - 1,)),
            dma((2,)), dma((2,)),
            dma((1,)), dma((1,)),
            dma((3,)), dma((3,)),
        ],
        compiler_params=pltpu.CompilerParams(
            collective_id=0, has_side_effects=True, vmem_limit_bytes=56 << 20
        ),
    )(slot_row[0, 0], slot_col[0, 0], counts, start_block, blocks[0, 0])
    return pl.pallas_call(
        finish,
        out_shape=(
            jax.ShapeDtypeStruct((2, k, k), F32),
            jax.ShapeDtypeStruct((2, k, k), F32),
            jax.ShapeDtypeStruct((piece, k, orb), F32),
        ),
        in_specs=[vmem],
        out_specs=(vmem, vmem, vmem),
    )(pltpu.with_memory_space_constraint(packed, pltpu.VMEM))


def solution(mesh):
    placed = (
        P(("row", "col"), None, None),
        P("row", "col", None, None, None),
        P("row", "col", None),
        P("row", "col", None),
        P("row", "col"),
    )
    return jax.shard_map(
        functools.partial(on_device, mesh.shape["row"], mesh.shape["col"]),
        mesh=mesh,
        in_specs=placed,
        out_specs=(P(), P(), P(("row", "col"), None, None)),
        check_vma=False,
    )
```
